256 devices in a mesh: dp: 32 (over y, z), tensor: 8 (over x, core).
Axes of the slice: x: 4, y: 4, z: 8, core: 2. Of those that a mesh axis runs over, the one named last changes fastest.
Arguments:
- queries: bfloat16 [256, 6, 8192], P('dp', None, 'tensor'), may hold values from -150 to 150
- new_keys: bfloat16 [256, 6, 1024], P('dp', None, 'tensor'), may hold values from -6 to 6
- new_values: bfloat16 [256, 6, 1024], P('dp', None, 'tensor'), may hold values from -6 to 6
- key_cache: bfloat16 [256, 256, 1024], P('dp', None, 'tensor'), may hold values from -6 to 6
- value_cache: bfloat16 [256, 256, 1024], P('dp', None, 'tensor'), may hold values from -6 to 6
- cache_lengths: int32 [256], P('dp'), may hold values from 32 to 256, as said below
- accepted: int32 [256], P('tensor'), may hold values from 1 to 6
- residual: bfloat16 [256, 6, 8192], P('tensor', None, 'dp'), may hold values from -6 to 6
- out_weight: bfloat16 [8192, 8192], P('tensor', 'dp'), may hold values from -0.0625 to 0.0625
- draft_weight: bfloat16 [8192, 8192], P('tensor', 'dp'), may hold values from -0.0625 to 0.0625
Outputs:
- verified: bfloat16 [256, 6, 8192], P('tensor', None, 'dp')
- drafted: bfloat16 [5, 256, 8192], P(None, 'tensor', 'dp')
The draws below stay inside these ranges and needn't reach their ends.
Inputs may be any that keep to these rules, and one draw needn't show every extreme that they name: `cache_lengths`: every draw has a window with all 256 slots live.
All inputs are finite; a program needn't handle non-finite values.
Results may differ from the reference program's by a relative error of at most 0.008.
Values may be sent and summed in bfloat16 or wider, within the bound.
No kernel may reach another device: no remote copies, remote signals or barrier semaphores. Data moves between devices by JAX's collectives and lax.ppermute only.
A program may use at most 64 MiB of HBM per device.

```python
import jax
import jax.numpy as jnp
from jax import lax

D = 8192
HD = 128
HEADS = 64
KVH = 8
Q = 6
STEPS = 5
CACHE = 256
WINDOWS = 256


def cache_base(key):
    return jnp.clip(jax.random.normal(jax.random.fold_in(key, 11), (WINDOWS, CACHE, KVH * HD), jnp.float32), -6.0, 6.0)


def draw_key_cache(key, part):
    base = cache_base(key)
    return base.astype(jnp.bfloat16)


def draw_queries(key, part):
    values = jnp.clip(jax.random.normal(jax.random.fold_in(key, 12), (WINDOWS, Q, HEADS * HD), jnp.float32), -6.0, 6.0)
    return values.astype(jnp.bfloat16)


def draw_cache_lengths(key, part):
    lengths = jax.random.randint(jax.random.fold_in(key, 13), (WINDOWS,), CACHE // 8, CACHE + 1, dtype=jnp.int32)
    return lengths.at[0].set(CACHE)


def place_ends(values, own_key, low, high):
    longest = values.shape.index(max(values.shape))
    spots = []
    for shift in (0, 1):
        where = [jax.random.randint(jax.random.fold_in(own_key, axis), (), 0, length) for axis, length in enumerate(values.shape)]
        where[longest] = (where[longest] + shift) % values.shape[longest]
        spots.append(tuple(where))
    return values.at[spots[0]].set(low).at[spots[1]].set(high)


def shard_levels(own_key, shape, shards, smallest, high):
    def one(position, blocks):
        steps = jax.random.uniform(jax.random.fold_in(jax.random.fold_in(own_key, 6), position), (blocks,), jnp.float32, smallest / len(shards), high / len(shards))
        return jnp.repeat(jnp.exp(steps), shape[position] // blocks).reshape((-1,) + (1,) * (len(shape) - position - 1))

    loudness = one(*shards[0])
    for cut in shards[1:]:
        loudness = loudness * one(*cut)
    return loudness


def noise(stream_key, extent, width, most, split=(), held_as=jnp.bfloat16):
    entries = jax.random.normal(stream_key, extent, jnp.float32) * width
    if len(split) > 0:
        entries = shard_levels(stream_key, extent, split, -0.22, 0.18) * entries
    return jnp.clip(entries, min=-most, max=most).astype(held_as)


def setup_inputs(seed: int = 0) -> dict:
    seeds = jax.random.split(jax.random.key(seed), 11)
    return {
        "queries": draw_queries(jax.random.fold_in(seeds[10], 71), 0),
        "new_keys": noise(seeds[1], (WINDOWS, Q, KVH * HD), 1.0, 6.0, ((0, 32), (2, 8))),
        "new_values": noise(seeds[2], (WINDOWS, Q, KVH * HD), 1.0, 6.0, ((0, 32), (2, 8))),
        "key_cache": draw_key_cache(jax.random.fold_in(seeds[10], 71), 0),
        "value_cache": noise(seeds[4], (WINDOWS, CACHE, KVH * HD), 1.0, 6.0, ((0, 32), (2, 8))),
        "cache_lengths": draw_cache_lengths(jax.random.fold_in(seeds[10], 71), 0),
        "accepted": place_ends(jax.random.randint(seeds[6], (WINDOWS,), 1, Q + 1), jax.random.fold_in(seeds[6], 1), 1, Q).astype(jnp.int32),
        "residual": noise(seeds[7], (WINDOWS, Q, D), 1.0, 6.0, ((0, 8), (2, 32))),
        "out_weight": noise(seeds[8], (HEADS * HD, D), (HEADS * HD) ** -0.5, 0.0625, ((0, 8), (1, 32))),
        "draft_weight": noise(seeds[9], (D, D), D ** -0.5, 0.0625, ((0, 8), (1, 32))),
    }


def attend_window(packed):
    query_rows, fresh_keys, fresh_values, cache_keys, cache_values, length = packed
    group_size = HEADS // KVH
    query_float = query_rows.astype(jnp.float32).reshape(Q, KVH, group_size, HD)
    keys_cached = cache_keys.astype(jnp.float32).reshape(CACHE, KVH, HD)
    keys_fresh = fresh_keys.astype(jnp.float32).reshape(Q, KVH, HD)
    score_cache = jnp.einsum("tkgd,pkd->kgtp", query_float, keys_cached) * (HD ** -0.5)
    score_fresh = jnp.einsum("tkgd,pkd->kgtp", query_float, keys_fresh) * (HD ** -0.5)
    live_cache = jnp.arange(CACHE) < length
    live_fresh = jnp.arange(Q)[None, :] <= jnp.arange(Q)[:, None]
    scores = jnp.concatenate([jnp.where(live_cache, score_cache, -jnp.inf), jnp.where(live_fresh, score_fresh, -jnp.inf)], axis=-1)
    largest = jnp.max(scores, axis=-1, keepdims=True)
    powered = jnp.exp(scores - largest)
    weights = (powered / jnp.sum(powered, axis=-1, keepdims=True)).astype(jnp.bfloat16).astype(jnp.float32)
    values_cached = cache_values.astype(jnp.float32).reshape(CACHE, KVH, HD)
    values_fresh = fresh_values.astype(jnp.float32).reshape(Q, KVH, HD)
    mixed_rows = jnp.einsum("kgtp,pkd->tkgd", weights[..., :CACHE], values_cached) + jnp.einsum("kgtp,pkd->tkgd", weights[..., CACHE:], values_fresh)
    return mixed_rows.reshape(Q, HEADS * HD).astype(jnp.bfloat16)


def reference(queries, new_keys, new_values, key_cache, value_cache, cache_lengths, accepted, residual, out_weight, draft_weight):
    attended = lax.map(attend_window, (queries, new_keys, new_values, key_cache, value_cache, cache_lengths))
    flat_rows = attended.reshape(WINDOWS * Q, HEADS * HD)
    projected = jnp.dot(flat_rows, out_weight, preferred_element_type=jnp.float32)
    verified = (residual.reshape(WINDOWS * Q, D).astype(jnp.float32) + projected).astype(jnp.bfloat16).reshape(WINDOWS, Q, D)
    feature = verified[jnp.arange(WINDOWS), accepted - 1]
    results = []
    for draft_step in range(STEPS):
        feature = jnp.tanh(2.0 * jnp.dot(feature, draft_weight, preferred_element_type=jnp.float32)).astype(jnp.bfloat16)
        results.append(feature)
    return verified, jnp.stack(results)
```

```python
import jax
import jax.numpy as jnp
from jax import lax
from jax.sharding import PartitionSpec as P

HD = 128
STEPS = 5


def spread(block, axis):
    copies = jnp.broadcast_to(block[None], (lax.axis_size(axis),) + block.shape)
    return lax.all_to_all(copies, axis, split_axis=0, concat_axis=0, tiled=True)


def accepted_of_my_windows(accepted):
    dp_size, tensor_size = lax.axis_size("dp"), lax.axis_size("tensor")
    ratio = dp_size // tensor_size
    pairs = []
    for j in range(dp_size):
        for i in range(tensor_size):
            source = (ratio * i + j % ratio) * tensor_size + j // ratio
            pairs.append((source, j * tensor_size + i))
    block = lax.ppermute(accepted, ("dp", "tensor"), pairs)
    rows = accepted.shape[0] // ratio
    return lax.dynamic_slice_in_dim(block, lax.axis_index("dp") % ratio * rows, rows, 0)


def pick(rows, accepted):
    chosen = jnp.arange(rows.shape[1])[None, :] == (accepted - 1)[:, None]
    return jnp.sum(
        jnp.where(chosen[:, :, None], rows, jnp.zeros((), rows.dtype)), axis=1, dtype=rows.dtype
    )


def per_device(
    queries,
    new_keys,
    new_values,
    key_cache,
    value_cache,
    cache_lengths,
    accepted,
    residual,
    out_weight,
    draft_weight,
):
    windows_here, tokens_here, query_width = queries.shape
    cache_size = key_cache.shape[1]
    kv_here = new_keys.shape[2] // HD
    group_size = query_width // HD // kv_here
    tensor_size = lax.axis_size("tensor")
    own_accepted = accepted_of_my_windows(accepted)
    draft_columns = lax.all_gather(draft_weight, "tensor", axis=0, tiled=True)

    query_split = queries.reshape(windows_here, tokens_here, kv_here, group_size, HD)
    keys_cached = key_cache.reshape(windows_here, cache_size, kv_here, HD)
    keys_fresh = new_keys.reshape(windows_here, tokens_here, kv_here, HD)
    score_cache = jnp.einsum(
        "wtkgd,wpkd->wkgtp", query_split, keys_cached, preferred_element_type=jnp.float32
    ) * HD ** (-0.5)
    score_fresh = jnp.einsum(
        "wtkgd,wpkd->wkgtp", query_split, keys_fresh, preferred_element_type=jnp.float32
    ) * HD ** (-0.5)
    live_cache = (jnp.arange(cache_size)[None, :] < cache_lengths[:, None])[:, None, None, None, :]
    live_fresh = jnp.arange(tokens_here)[None, :] <= jnp.arange(tokens_here)[:, None]
    scores = jnp.concatenate(
        [
            jnp.where(live_cache, score_cache, -jnp.inf),
            jnp.where(live_fresh, score_fresh, -jnp.inf),
        ],
        axis=-1,
    )
    largest = jnp.max(scores, axis=-1, keepdims=True)
    powered = jnp.exp(scores - largest)
    weights = (powered / jnp.sum(powered, axis=-1, keepdims=True)).astype(jnp.bfloat16)
    values_cached = value_cache.reshape(windows_here, cache_size, kv_here, HD)
    values_fresh = new_values.reshape(windows_here, tokens_here, kv_here, HD)
    mixed_rows = jnp.einsum(
        "wkgtp,wpkd->wtkgd",
        weights[..., :cache_size],
        values_cached,
        preferred_element_type=jnp.float32,
    )
    mixed_rows = mixed_rows + jnp.einsum(
        "wkgtp,wpkd->wtkgd",
        weights[..., cache_size:],
        values_fresh,
        preferred_element_type=jnp.float32,
    )
    attended = mixed_rows.astype(jnp.bfloat16).reshape(windows_here, tokens_here, query_width)

    picked_rows = spread(pick(attended, own_accepted), "dp").reshape(-1, query_width)
    picked_part = jnp.dot(picked_rows, out_weight, preferred_element_type=jnp.float32)
    block_windows, block_tokens, block_cols = residual.shape
    shares = lax.all_to_all(
        picked_part.astype(jnp.bfloat16).reshape(tensor_size, block_windows, block_cols),
        "tensor",
        split_axis=0,
        concat_axis=0,
        tiled=True,
    )
    current = (
        pick(residual, accepted).astype(jnp.float32) + jnp.sum(shares.astype(jnp.float32), axis=0)
    ).astype(jnp.bfloat16)

    partial_out = jnp.dot(
        lax.all_gather(
            attended.reshape(windows_here * tokens_here, query_width), "dp", axis=0, tiled=True
        ),
        out_weight,
        preferred_element_type=jnp.float32,
    )
    summed = lax.psum_scatter(partial_out, "tensor", scatter_dimension=0, tiled=True)
    flat_residual = residual.reshape(block_windows * block_tokens, block_cols).astype(jnp.float32)
    verified = (
        (flat_residual + summed)
        .astype(jnp.bfloat16)
        .reshape(block_windows, block_tokens, block_cols)
    )

    columns = draft_columns.reshape(-1, block_cols, draft_columns.shape[1])
    results = []
    for draft_step in range(STEPS):
        inputs = spread(current, "dp")
        product = jnp.einsum("jwk,jkn->wn", inputs, columns, preferred_element_type=jnp.float32)
        current = jnp.tanh(2.0 * product).astype(jnp.bfloat16)
        results.append(current)
    return (verified, jnp.stack(results))


def solution(mesh):
    placed = (
        P("dp", None, "tensor"),
        P("dp", None, "tensor"),
        P("dp", None, "tensor"),
        P("dp", None, "tensor"),
        P("dp", None, "tensor"),
        P("dp"),
        P("tensor"),
        P("tensor", None, "dp"),
        P("tensor", "dp"),
        P("tensor", "dp"),
    )
    return jax.shard_map(
        per_device,
        mesh=mesh,
        in_specs=placed,
        out_specs=(P("tensor", None, "dp"), P(None, "tensor", "dp")),
        check_vma=False,
    )
```

```python
import jax
import jax.numpy as jnp
from jax import lax
from jax.experimental import pallas as pl
from jax.experimental.pallas import tpu as pltpu
from jax.sharding import PartitionSpec as P

HD = 128
STEPS = 5
HOLD = 2


def spread(block, axis):
    copies = jnp.broadcast_to(block[None], (lax.axis_size(axis),) + block.shape)
    return lax.all_to_all(copies, axis, split_axis=0, concat_axis=0, tiled=True)


Y, ZH, ZL, X, C = 4, 2, 4, 4, 2
BLOCKS = [[(y * ZH + zh) * ZL + zl for y in range(Y) for zl in range(ZL)] for zh in range(ZH)]


def route(source):
    pairs = []
    for y in range(Y):
        for zh in range(ZH):
            for zl in range(ZL):
                for x in range(X):
                    for c in range(C):
                        ends = []
                        for sy, szh, szl, sx, sc in (source(y, zh, zl, x, c), (y, zh, zl, x, c)):
                            ends.append((((sy * ZH + szh) * ZL + szl) * X + sx) * C + sc)
                        pairs.append(tuple(ends))
    return pairs


SWAPPED = route(lambda y, zh, zl, x, c: (y, c, zl, x, zh))
SWAPPED_OTHER = route(lambda y, zh, zl, x, c: (y, c, zl, x, 1 - zh))
OTHER_CORE = route(lambda y, zh, zl, x, c: (y, zh, zl, x, 1 - c))
X_BEHIND = [route(lambda y, zh, zl, x, c, s=s: (y, zh, zl, (x - s) % X, c)) for s in range(X)]


def move(block, pairs):
    return lax.ppermute(block, ("dp", "tensor"), pairs)


def draft_weights(shard):
    here = move(shard, SWAPPED)
    there = move(shard, SWAPPED_OTHER)
    same = lax.axis_index("dp") // ZL % ZH == lax.axis_index("tensor") % C
    both = jnp.stack([jnp.where(same, here, there), jnp.where(same, there, here)])
    return [both] + [move(both, X_BEHIND[s]) for s in range(1, X)]


def draft_kernel(own_ref, other_ref, *refs):
    weight_refs, (drafted_ref, copies_ref) = refs[:X], refs[X:]
    x = lax.axis_index("tensor") // C
    total = jnp.zeros(drafted_ref.shape, jnp.float32)
    depth = own_ref.shape[2]
    for s in range(X):
        y = lax.rem(x + X - s, X)
        for half, rows_ref in enumerate((own_ref, other_ref)):
            for zl in range(ZL):
                total += jnp.dot(
                    rows_ref[y * ZL + zl],
                    weight_refs[s][half, zl * depth : (zl + 1) * depth, :],
                    preferred_element_type=jnp.float32,
                )
    drafted = jnp.tanh(2.0 * total).astype(drafted_ref.dtype)
    drafted_ref[...] = drafted
    for copy in range(copies_ref.shape[0]):
        copies_ref[copy] = drafted


def draft_step(own, other, weights):
    count, rows, cols = own.shape
    return pl.pallas_call(
        draft_kernel,
        out_shape=(
            jax.ShapeDtypeStruct((rows, cols), own.dtype),
            jax.ShapeDtypeStruct((count, rows, cols), own.dtype),
        ),
        in_specs=[pl.BlockSpec(memory_space=pltpu.VMEM)] * (2 + X),
        out_specs=(pl.BlockSpec(memory_space=pltpu.VMEM),) * 2,
        compiler_params=pltpu.CompilerParams(vmem_limit_bytes=24 << 20),
        cost_estimate=pl.CostEstimate(
            flops=4 * count * rows * cols * cols,
            bytes_accessed=4 * count * cols * cols + 6 * count * rows * cols,
            transcendentals=rows * cols,
        ),
        name="draft_step",
    )(own, other, *weights)


def accepted_of_my_windows(accepted):
    everyone = spread(accepted, "tensor").reshape(-1)
    rows = everyone.shape[0] // lax.axis_size("dp")
    return lax.dynamic_slice_in_dim(everyone, lax.axis_index("dp") * rows, rows, 0)


def pick(rows, accepted):
    chosen = jnp.arange(rows.shape[1])[None, :] == (accepted - 1)[:, None]
    return jnp.sum(
        jnp.where(chosen[:, :, None], rows, jnp.zeros((), rows.dtype)), axis=1, dtype=rows.dtype
    )


def per_device(
    queries,
    new_keys,
    new_values,
    key_cache,
    value_cache,
    cache_lengths,
    accepted,
    residual,
    out_weight,
    draft_weight,
):
    windows_here, tokens_here, query_width = queries.shape
    cache_size = key_cache.shape[1]
    kv_here = new_keys.shape[2] // HD
    group_size = query_width // HD // kv_here
    tensor_size = lax.axis_size("tensor")
    own_accepted = accepted_of_my_windows(accepted)
    weights_moved = draft_weights(draft_weight)

    query_split = queries.reshape(windows_here, tokens_here, kv_here, group_size, HD)
    keys_cached = key_cache.reshape(windows_here, cache_size, kv_here, HD)
    keys_fresh = new_keys.reshape(windows_here, tokens_here, kv_here, HD)
    score_cache = jnp.einsum(
        "wtkgd,wpkd->wkgtp", query_split, keys_cached, preferred_element_type=jnp.float32
    ) * HD ** (-0.5)
    score_fresh = jnp.einsum(
        "wtkgd,wpkd->wkgtp", query_split, keys_fresh, preferred_element_type=jnp.float32
    ) * HD ** (-0.5)
    live_cache = (jnp.arange(cache_size)[None, :] < cache_lengths[:, None])[:, None, None, None, :]
    live_fresh = jnp.arange(tokens_here)[None, :] <= jnp.arange(tokens_here)[:, None]
    scores = jnp.concatenate(
        [
            jnp.where(live_cache, score_cache, -jnp.inf),
            jnp.where(live_fresh, score_fresh, -jnp.inf),
        ],
        axis=-1,
    )
    largest = jnp.max(scores, axis=-1, keepdims=True)
    powered = jnp.exp(scores - largest)
    weights = (powered / jnp.sum(powered, axis=-1, keepdims=True)).astype(jnp.bfloat16)
    values_cached = value_cache.reshape(windows_here, cache_size, kv_here, HD)
    values_fresh = new_values.reshape(windows_here, tokens_here, kv_here, HD)
    mixed_rows = jnp.einsum(
        "wkgtp,wpkd->wtkgd",
        weights[..., :cache_size],
        values_cached,
        preferred_element_type=jnp.float32,
    )
    mixed_rows = mixed_rows + jnp.einsum(
        "wkgtp,wpkd->wtkgd",
        weights[..., cache_size:],
        values_fresh,
        preferred_element_type=jnp.float32,
    )
    attended = mixed_rows.astype(jnp.bfloat16).reshape(windows_here, tokens_here, query_width)

    picked_rows = spread(pick(attended, own_accepted), "dp").reshape(-1, query_width)
    picked_part = jnp.dot(picked_rows, out_weight, preferred_element_type=jnp.float32)
    block_windows, block_tokens, block_cols = residual.shape
    shares = lax.all_to_all(
        picked_part.astype(jnp.bfloat16).reshape(tensor_size, block_windows, block_cols),
        "tensor",
        split_axis=0,
        concat_axis=0,
        tiled=True,
    )
    current = (
        pick(residual, accepted).astype(jnp.float32) + jnp.sum(shares.astype(jnp.float32), axis=0)
    ).astype(jnp.bfloat16)

    gathered = lax.all_gather(
        attended.reshape(windows_here * tokens_here, query_width), "dp", axis=0, tiled=True
    )

    current = move(current, SWAPPED)
    copies = jnp.broadcast_to(current[None], (len(BLOCKS[0]),) + current.shape)
    results = []
    for step in range(STEPS):
        own = lax.all_to_all(
            copies, "dp", split_axis=0, concat_axis=0, tiled=True, axis_index_groups=BLOCKS
        )
        other = move(own, OTHER_CORE)
        drafted, copies = draft_step(own, other, weights_moved)
        results.append(move(drafted, SWAPPED))
        if step == HOLD:
            gathered, copies = lax.optimization_barrier((gathered, copies))

    partial_out = jnp.dot(gathered, out_weight, preferred_element_type=jnp.float32)
    parts = lax.all_to_all(
        partial_out.astype(jnp.bfloat16).reshape(
            tensor_size, block_windows * block_tokens, block_cols
        ),
        "tensor",
        split_axis=0,
        concat_axis=0,
        tiled=True,
    )
    summed = jnp.sum(parts.astype(jnp.float32), axis=0).reshape(residual.shape)
    verified = (residual.astype(jnp.float32) + summed).astype(jnp.bfloat16)
    return (verified, jnp.stack(results))


def solution(mesh):
    placed = (
        P("dp", None, "tensor"),
        P("dp", None, "tensor"),
        P("dp", None, "tensor"),
        P("dp", None, "tensor"),
        P("dp", None, "tensor"),
        P("dp"),
        P("tensor"),
        P("tensor", None, "dp"),
        P("tensor", "dp"),
        P("tensor", "dp"),
    )
    return jax.shard_map(
        per_device,
        mesh=mesh,
        in_specs=placed,
        out_specs=(P("tensor", None, "dp"), P(None, "tensor", "dp")),
        check_vma=False,
    )
```

```python
import functools

import jax
import jax.numpy as jnp
from jax import lax
from jax.experimental import pallas as pl
from jax.experimental.pallas import tpu as pltpu
from jax.sharding import PartitionSpec as P

HD = 128
STEPS = 5
HOLD = 2


def spread(block, axis):
    copies = jnp.broadcast_to(block[None], (lax.axis_size(axis),) + block.shape)
    return lax.all_to_all(copies, axis, split_axis=0, concat_axis=0, tiled=True)


YH, YL, Z, X, C = 2, 2, 8, 4, 2
BLOCKS = [list(range(yh * YL * Z, (yh + 1) * YL * Z)) for yh in range(YH)]


def route(source):
    pairs = []
    for yh in range(YH):
        for yl in range(YL):
            for z in range(Z):
                for x in range(X):
                    for c in range(C):
                        ends = []
                        for syh, sx, sc in (source(yh, x, c), (yh, x, c)):
                            ends.append((((syh * YL + yl) * Z + z) * X + sx % X) * C + sc)
                        pairs.append(tuple(ends))
    return pairs


SWAPPED = route(lambda yh, x, c: (c, x, yh))
SWAPPED_OTHER = route(lambda yh, x, c: (c, x, 1 - yh))
OTHER_CORE = route(lambda yh, x, c: (yh, x, 1 - c))
FROM_LEFT = route(lambda yh, x, c: (yh, x - 1, c))
FROM_RIGHT = route(lambda yh, x, c: (yh, x + 1, c))


def move(block, pairs):
    return lax.ppermute(block, ("dp", "tensor"), pairs)


def draft_kernel(own_ref, other_ref, here_ref, left_ref, right_ref, low_ref, high_ref, *refs, last, to_hbm):
    place = lax.axis_index("tensor")
    x, c = place // C, lax.rem(place, C)
    count, height, cols = own_ref.shape
    if last:
        *earlier_refs, stack_ref, rows_ref = refs
    elif to_hbm:
        drafted_ref, copies_hbm_ref, rows_ref, copies_ref, sem = refs
    else:
        drafted_ref, copies_ref, rows_ref = refs
    for k in range(count):
        rows_ref[c * count + k] = own_ref[k]
        rows_ref[(1 - c) * count + k] = other_ref[k]
    total = jnp.zeros((height, cols), jnp.float32)
    per_x = rows_ref.shape[0] // X
    half = per_x // 2
    for offset, shift, weight_ref in (
        (0, 0, here_ref),
        (X - 1, 0, left_ref),
        (1, 0, right_ref),
        (2, 0, low_ref),
        (2, half, high_ref),
    ):
        first = lax.rem(x + offset, X) * per_x + shift
        wide = jnp.concatenate(
            [rows_ref[first + k] for k in range(weight_ref.shape[0] // cols)], axis=1
        )
        total += jnp.dot(wide, weight_ref[...], preferred_element_type=jnp.float32)
    drafted = jnp.tanh(2.0 * total).astype(own_ref.dtype)
    if last:
        for k, earlier_ref in enumerate(earlier_refs):
            stack_ref[k] = earlier_ref[...]
        stack_ref[len(earlier_refs)] = drafted
        return
    drafted_ref[...] = drafted
    for copy in range(count):
        copies_ref[copy] = drafted
    if to_hbm:
        send = pltpu.make_async_copy(copies_ref, copies_hbm_ref, sem)
        send.start()
        send.wait()


def draft_step(own, other, weights, earlier, last, to_hbm):
    count, height, cols = own.shape
    vmem = pl.BlockSpec(memory_space=pltpu.VMEM)
    rows = pltpu.VMEM((2 * count, height, cols), own.dtype)
    block = jax.ShapeDtypeStruct((height, cols), own.dtype)
    copies = jax.ShapeDtypeStruct(own.shape, own.dtype)
    if last:
        operands = (own, other, *weights, *earlier)
        out_shape = jax.ShapeDtypeStruct((len(earlier) + 1, height, cols), own.dtype)
        out_specs, scratch = vmem, [rows]
    else:
        operands = (own, other, *weights)
        out_shape, out_specs, scratch = (block, copies), (vmem, vmem), [rows]
        if to_hbm:
            out_specs = (vmem, pl.BlockSpec(memory_space=pltpu.HBM))
            scratch = [rows, pltpu.VMEM(own.shape, own.dtype), pltpu.SemaphoreType.DMA]
    return pl.pallas_call(
        functools.partial(draft_kernel, last=last, to_hbm=to_hbm),
        out_shape=out_shape,
        in_specs=[vmem] * len(operands),
        out_specs=out_specs,
        scratch_shapes=scratch,
        compiler_params=pltpu.CompilerParams(vmem_limit_bytes=24 << 20),
        cost_estimate=pl.CostEstimate(
            flops=4 * count * height * cols * cols,
            bytes_accessed=4 * count * cols * cols + 6 * count * height * cols,
            transcendentals=height * cols,
        ),
        name="draft_step",
    )(*operands)


def accepted_of_my_windows(everyone):
    rows = everyone.shape[0] // lax.axis_size("dp")
    return lax.dynamic_slice_in_dim(everyone, lax.axis_index("dp") * rows, rows, 0)


def pick(rows, accepted):
    chosen = jnp.arange(rows.shape[1])[None, :] == (accepted - 1)[:, None]
    return jnp.sum(
        jnp.where(chosen[:, :, None], rows, jnp.zeros((), rows.dtype)), axis=1, dtype=rows.dtype
    )


def per_device(
    queries,
    new_keys,
    new_values,
    key_cache,
    value_cache,
    cache_lengths,
    accepted,
    residual,
    out_weight,
    draft_weight,
):
    windows_here, tokens_here, query_width = queries.shape
    cache_size = key_cache.shape[1]
    kv_here = new_keys.shape[2] // HD
    group_size = query_width // HD // kv_here
    tensor_size = lax.axis_size("tensor")
    everyone, swapped, swapped_other = lax.optimization_barrier(
        (
            spread(accepted, "tensor").reshape(-1),
            move(draft_weight, SWAPPED),
            move(draft_weight, SWAPPED_OTHER),
        )
    )
    own_accepted = accepted_of_my_windows(everyone)

    query_split = queries.reshape(windows_here, tokens_here, kv_here, group_size, HD)
    keys_cached = key_cache.reshape(windows_here, cache_size, kv_here, HD)
    keys_fresh = new_keys.reshape(windows_here, tokens_here, kv_here, HD)
    score_cache = jnp.einsum(
        "wtkgd,wpkd->wkgtp", query_split, keys_cached, preferred_element_type=jnp.float32
    ) * HD ** (-0.5)
    score_fresh = jnp.einsum(
        "wtkgd,wpkd->wkgtp", query_split, keys_fresh, preferred_element_type=jnp.float32
    ) * HD ** (-0.5)
    live_cache = (jnp.arange(cache_size)[None, :] < cache_lengths[:, None])[:, None, None, None, :]
    live_fresh = jnp.arange(tokens_here)[None, :] <= jnp.arange(tokens_here)[:, None]
    scores = jnp.concatenate(
        [
            jnp.where(live_cache, score_cache, -jnp.inf),
            jnp.where(live_fresh, score_fresh, -jnp.inf),
        ],
        axis=-1,
    )
    largest = jnp.max(scores, axis=-1, keepdims=True)
    powered = jnp.exp(scores - largest)
    weights = (powered / jnp.sum(powered, axis=-1, keepdims=True)).astype(jnp.bfloat16)
    values_cached = value_cache.reshape(windows_here, cache_size, kv_here, HD)
    values_fresh = new_values.reshape(windows_here, tokens_here, kv_here, HD)
    mixed_rows = jnp.einsum(
        "wkgtp,wpkd->wtkgd",
        weights[..., :cache_size],
        values_cached,
        preferred_element_type=jnp.float32,
    )
    mixed_rows = mixed_rows + jnp.einsum(
        "wkgtp,wpkd->wtkgd",
        weights[..., cache_size:],
        values_fresh,
        preferred_element_type=jnp.float32,
    )
    attended = mixed_rows.astype(jnp.bfloat16).reshape(windows_here, tokens_here, query_width)

    picked = pick(attended, own_accepted)
    low_half = lax.axis_index("dp") < YL * Z
    here = jnp.concatenate(
        [
            jnp.where(low_half, swapped, swapped_other),
            jnp.where(low_half, swapped_other, swapped),
        ]
    )
    left, right = move(here, FROM_LEFT), move(here, FROM_RIGHT)
    picked_rows = spread(picked, "dp").reshape(-1, query_width)
    picked_part = jnp.dot(picked_rows, out_weight, preferred_element_type=jnp.float32)
    block_windows, block_tokens, block_cols = residual.shape
    shares = lax.all_to_all(
        picked_part.astype(jnp.bfloat16).reshape(tensor_size, block_windows, block_cols),
        "tensor",
        split_axis=0,
        concat_axis=0,
        tiled=True,
    )
    shares, left, right = lax.optimization_barrier((shares, left, right))
    low = move(left[: left.shape[0] // 2], FROM_LEFT)
    high = move(right[right.shape[0] // 2 :], FROM_RIGHT)
    current = (
        pick(residual, accepted).astype(jnp.float32) + jnp.sum(shares.astype(jnp.float32), axis=0)
    ).astype(jnp.bfloat16)

    gathered = lax.all_gather(
        attended.reshape(windows_here * tokens_here, query_width), "dp", axis=0, tiled=True
    )

    current = move(current, SWAPPED)
    copies = jnp.broadcast_to(current[None], (len(BLOCKS[0]),) + current.shape)
    weights = (here, left, right, low, high)
    results = []
    for step in range(STEPS):
        own = lax.all_to_all(
            copies, "dp", split_axis=0, concat_axis=0, tiled=True, axis_index_groups=BLOCKS
        )
        other = move(own, OTHER_CORE)
        last = step + 1 == STEPS
        drafted = draft_step(own, other, weights, results, last, step == HOLD)
        if last:
            break
        drafted, copies = drafted
        results.append(drafted)
        if step == HOLD:
            gathered, copies = lax.optimization_barrier((gathered, copies))
    partial_out = jnp.dot(gathered, out_weight, preferred_element_type=jnp.float32)
    summed = lax.psum_scatter(partial_out, "tensor", scatter_dimension=0, tiled=True)
    drafted, summed = lax.optimization_barrier((drafted, summed))
    verified = (residual.astype(jnp.float32) + summed.reshape(residual.shape)).astype(jnp.bfloat16)
    return (verified, move(drafted, SWAPPED))


def solution(mesh):
    placed = (
        P("dp", None, "tensor"),
        P("dp", None, "tensor"),
        P("dp", None, "tensor"),
        P("dp", None, "tensor"),
        P("dp", None, "tensor"),
        P("dp"),
        P("tensor"),
        P("tensor", None, "dp"),
        P("tensor", "dp"),
        P("tensor", "dp"),
    )
    return jax.shard_map(
        per_device,
        mesh=mesh,
        in_specs=placed,
        out_specs=(P("tensor", None, "dp"), P(None, "tensor", "dp")),
        check_vma=False,
    )
```

```python
import functools

import jax
import jax.numpy as jnp
from jax import lax
from jax.experimental import pallas as pl
from jax.experimental.pallas import tpu as pltpu
from jax.sharding import PartitionSpec as P

HD = 128
STEPS = 5
HOLD = 1


def spread(block, axis):
    copies = jnp.broadcast_to(block[None], (lax.axis_size(axis),) + block.shape)
    return lax.all_to_all(copies, axis, split_axis=0, concat_axis=0, tiled=True)


YH, YL, Z, X, C = 2, 2, 8, 4, 2
BLOCKS = [list(range(yh * YL * Z, (yh + 1) * YL * Z)) for yh in range(YH)]


def route(source):
    pairs = []
    for yh in range(YH):
        for yl in range(YL):
            for z in range(Z):
                for x in range(X):
                    for c in range(C):
                        ends = []
                        for syh, sx, sc in (source(yh, x, c), (yh, x, c)):
                            ends.append((((syh * YL + yl) * Z + z) * X + sx % X) * C + sc)
                        pairs.append(tuple(ends))
    return pairs


SWAPPED = route(lambda yh, x, c: (c, x, yh))
SWAPPED_OTHER = route(lambda yh, x, c: (c, x, 1 - yh))
OTHER_CORE = route(lambda yh, x, c: (yh, x, 1 - c))
FROM_LEFT = route(lambda yh, x, c: (yh, x - 1, c))
FROM_RIGHT = route(lambda yh, x, c: (yh, x + 1, c))


def move(block, pairs):
    return lax.ppermute(block, ("dp", "tensor"), pairs)


def exchange_copies(copies):
    return lax.all_to_all(
        copies, "dp", split_axis=0, concat_axis=0, tiled=True, axis_index_groups=BLOCKS
    )


def draft_kernel(own_ref, other_ref, *refs, last):
    place = lax.axis_index("tensor")
    x, c = place // C, lax.rem(place, C)
    count, height, cols = own_ref.shape
    weight_refs, refs = refs[: 2 * X], refs[2 * X :]
    if last:
        *earlier_refs, stack_ref, rows_ref = refs
    else:
        drafted_ref, copies_ref, *kept_refs, rows_ref = refs
    for k in range(count):
        rows_ref[c * count + k] = own_ref[k]
        rows_ref[(1 - c) * count + k] = other_ref[k]
    total = jnp.zeros((height, cols), jnp.float32)
    per_x = rows_ref.shape[0] // X
    half = per_x // 2
    for piece, weight_ref in enumerate(weight_refs):
        offset = (0, X - 1, 1, 2)[piece // 2]
        first = lax.rem(x + offset, X) * per_x + piece % 2 * half
        wide = jnp.concatenate(
            [rows_ref[first + k] for k in range(weight_ref.shape[0] // cols)], axis=1
        )
        total += jnp.dot(wide, weight_ref[...], preferred_element_type=jnp.float32)
    drafted = jnp.tanh(2.0 * total).astype(own_ref.dtype)
    if last:
        for k, earlier_ref in enumerate(earlier_refs):
            stack_ref[k] = earlier_ref[...]
        stack_ref[len(earlier_refs)] = drafted
        return
    drafted_ref[...] = drafted
    for copy in range(count):
        copies_ref[copy] = drafted
    for kept_ref, weight_ref in zip(kept_refs, weight_refs[X:]):
        kept_ref[...] = weight_ref[...]


def draft_step(own, other, weights, earlier, last, keep):
    count, height, cols = own.shape
    vmem = pl.BlockSpec(memory_space=pltpu.VMEM)
    rows = pltpu.VMEM((2 * count, height, cols), own.dtype)
    block = jax.ShapeDtypeStruct((height, cols), own.dtype)
    copies = jax.ShapeDtypeStruct(own.shape, own.dtype)
    if last:
        operands = (own, other, *weights, *earlier)
        out_shape = jax.ShapeDtypeStruct((len(earlier) + 1, height, cols), own.dtype)
        out_specs, scratch = vmem, [rows]
    else:
        operands = (own, other, *weights)
        kept = [jax.ShapeDtypeStruct(piece.shape, piece.dtype) for piece in weights[X:]]
        out_shape, scratch = [block, copies] + (kept if keep else []), [rows]
        out_specs = [vmem] * len(out_shape)
    return pl.pallas_call(
        functools.partial(draft_kernel, last=last),
        out_shape=out_shape,
        in_specs=[vmem] * len(operands),
        out_specs=out_specs,
        scratch_shapes=scratch,
        compiler_params=pltpu.CompilerParams(vmem_limit_bytes=8 << 20),
        cost_estimate=pl.CostEstimate(
            flops=4 * count * height * cols * cols,
            bytes_accessed=4 * count * cols * cols + 6 * count * height * cols,
            transcendentals=height * cols,
        ),
        name="draft_step",
    )(*operands)


def accepted_of_my_windows(everyone):
    rows = everyone.shape[0] // lax.axis_size("dp")
    return lax.dynamic_slice_in_dim(everyone, lax.axis_index("dp") * rows, rows, 0)


def pick(rows, accepted):
    chosen = jnp.arange(rows.shape[1])[None, :] == (accepted - 1)[:, None]
    return jnp.sum(
        jnp.where(chosen[:, :, None], rows, jnp.zeros((), rows.dtype)), axis=1, dtype=rows.dtype
    )


def per_device(
    queries,
    new_keys,
    new_values,
    key_cache,
    value_cache,
    cache_lengths,
    accepted,
    residual,
    out_weight,
    draft_weight,
):
    windows_here, tokens_here, query_width = queries.shape
    cache_size = key_cache.shape[1]
    kv_here = new_keys.shape[2] // HD
    group_size = query_width // HD // kv_here
    tensor_size = lax.axis_size("tensor")
    everyone, swapped, swapped_other = lax.optimization_barrier(
        (
            spread(accepted, "tensor").reshape(-1),
            move(draft_weight, SWAPPED),
            move(draft_weight, SWAPPED_OTHER),
        )
    )
    own_accepted = accepted_of_my_windows(everyone)

    query_split = queries.reshape(windows_here, tokens_here, kv_here, group_size, HD)
    keys_cached = key_cache.reshape(windows_here, cache_size, kv_here, HD)
    keys_fresh = new_keys.reshape(windows_here, tokens_here, kv_here, HD)
    score_cache = jnp.einsum(
        "wtkgd,wpkd->wkgtp", query_split, keys_cached, preferred_element_type=jnp.float32
    ) * HD ** (-0.5)
    score_fresh = jnp.einsum(
        "wtkgd,wpkd->wkgtp", query_split, keys_fresh, preferred_element_type=jnp.float32
    ) * HD ** (-0.5)
    live_cache = (jnp.arange(cache_size)[None, :] < cache_lengths[:, None])[:, None, None, None, :]
    live_fresh = jnp.arange(tokens_here)[None, :] <= jnp.arange(tokens_here)[:, None]
    scores = jnp.concatenate(
        [
            jnp.where(live_cache, score_cache, -jnp.inf),
            jnp.where(live_fresh, score_fresh, -jnp.inf),
        ],
        axis=-1,
    )
    largest = jnp.max(scores, axis=-1, keepdims=True)
    powered = jnp.exp(scores - largest)
    weights = (powered / jnp.sum(powered, axis=-1, keepdims=True)).astype(jnp.bfloat16)
    values_cached = value_cache.reshape(windows_here, cache_size, kv_here, HD)
    values_fresh = new_values.reshape(windows_here, tokens_here, kv_here, HD)
    mixed_rows = jnp.einsum(
        "wkgtp,wpkd->wtkgd",
        weights[..., :cache_size],
        values_cached,
        preferred_element_type=jnp.float32,
    )
    mixed_rows = mixed_rows + jnp.einsum(
        "wkgtp,wpkd->wtkgd",
        weights[..., cache_size:],
        values_fresh,
        preferred_element_type=jnp.float32,
    )
    attended = mixed_rows.astype(jnp.bfloat16).reshape(windows_here, tokens_here, query_width)

    picked = pick(attended, own_accepted)
    low_half = lax.axis_index("dp") < YL * Z
    top = jnp.where(low_half, swapped, swapped_other)
    bottom = jnp.where(low_half, swapped_other, swapped)
    top_left, bottom_right = move(top, FROM_LEFT), move(bottom, FROM_RIGHT)
    picked_rows = spread(picked, "dp").reshape(-1, query_width)
    bottom_left, top_right = move(bottom, FROM_LEFT), move(top, FROM_RIGHT)
    picked_part = jnp.dot(picked_rows, out_weight, preferred_element_type=jnp.float32)
    block_windows, block_tokens, block_cols = residual.shape
    shares = lax.all_to_all(
        picked_part.astype(jnp.bfloat16).reshape(tensor_size, block_windows, block_cols),
        "tensor",
        split_axis=0,
        concat_axis=0,
        tiled=True,
    )
    shares, top_left, bottom_left, top_right, bottom_right = lax.optimization_barrier(
        (shares, top_left, bottom_left, top_right, bottom_right)
    )
    top_across, bottom_across = move(top_left, FROM_LEFT), move(bottom_right, FROM_RIGHT)
    weights = (
        top, bottom, top_left, bottom_left, top_right, bottom_right, top_across, bottom_across
    )
    current = (
        pick(residual, accepted).astype(jnp.float32) + jnp.sum(shares.astype(jnp.float32), axis=0)
    ).astype(jnp.bfloat16)

    gathered = lax.all_gather(
        attended.reshape(windows_here * tokens_here, query_width), "dp", axis=0, tiled=True
    )

    current = move(current, SWAPPED)
    copies = jnp.broadcast_to(current[None], (len(BLOCKS[0]),) + current.shape)
    results = []
    for step in range(STEPS):
        own = exchange_copies(copies)
        if step == HOLD:
            gathered, own = lax.optimization_barrier((gathered, own))
        other = move(own, OTHER_CORE)
        last = step + 1 == STEPS
        drafted = draft_step(own, other, weights, results, last, step == HOLD)
        if last:
            break
        drafted, copies, *kept = drafted
        if kept:
            weights = (*weights[:X], *kept)
        results.append(drafted)
    partial_out = jnp.dot(gathered, out_weight, preferred_element_type=jnp.float32)
    summed = lax.psum_scatter(partial_out, "tensor", scatter_dimension=0, tiled=True)
    drafted, summed = lax.optimization_barrier((drafted, summed))
    verified = (residual.astype(jnp.float32) + summed.reshape(residual.shape)).astype(jnp.bfloat16)
    return (verified, move(drafted, SWAPPED))


def solution(mesh):
    placed = (
        P("dp", None, "tensor"),
        P("dp", None, "tensor"),
        P("dp", None, "tensor"),
        P("dp", None, "tensor"),
        P("dp", None, "tensor"),
        P("dp"),
        P("tensor"),
        P("tensor", None, "dp"),
        P("tensor", "dp"),
        P("tensor", "dp"),
    )
    return jax.shard_map(
        per_device,
        mesh=mesh,
        in_specs=placed,
        out_specs=(P("tensor", None, "dp"), P(None, "tensor", "dp")),
        check_vma=False,
    )
```

```python
import functools

import jax
import jax.numpy as jnp
from jax import lax
from jax.experimental import pallas as pl
from jax.experimental.pallas import tpu as pltpu
from jax.sharding import PartitionSpec as P

HD = 128
STEPS = 5
HOLD = 1


def spread(block, axis):
    copies = jnp.broadcast_to(block[None], (lax.axis_size(axis),) + block.shape)
    return lax.all_to_all(copies, axis, split_axis=0, concat_axis=0, tiled=True)


YH, YL, Z, X, C = 2, 2, 8, 4, 2
BLOCKS = [list(range(yh * YL * Z, (yh + 1) * YL * Z)) for yh in range(YH)]


def route(source):
    pairs = []
    for yh in range(YH):
        for yl in range(YL):
            for z in range(Z):
                for x in range(X):
                    for c in range(C):
                        ends = []
                        for syh, sx, sc in (source(yh, x, c), (yh, x, c)):
                            ends.append((((syh * YL + yl) * Z + z) * X + sx % X) * C + sc)
                        pairs.append(tuple(ends))
    return pairs


SWAPPED = route(lambda yh, x, c: (c, x, yh))
SWAPPED_OTHER = route(lambda yh, x, c: (c, x, 1 - yh))
OTHER_CORE = route(lambda yh, x, c: (yh, x, 1 - c))
FROM_LEFT = route(lambda yh, x, c: (yh, x - 1, c))
FROM_RIGHT = route(lambda yh, x, c: (yh, x + 1, c))


def move(block, pairs):
    return lax.ppermute(block, ("dp", "tensor"), pairs)


def exchange_copies(copies):
    return lax.all_to_all(
        copies, "dp", split_axis=0, concat_axis=0, tiled=True, axis_index_groups=BLOCKS
    )


def draft_kernel(own_ref, other_ref, *refs, last):
    place = lax.axis_index("tensor")
    x, c = place // C, lax.rem(place, C)
    count, height, cols = own_ref.shape
    weight_refs, refs = refs[: 2 * X], refs[2 * X :]
    if last:
        *earlier_refs, stack_ref, rows_ref = refs
    else:
        drafted_ref, copies_ref, *kept_refs, rows_ref = refs
    for k in range(count):
        rows_ref[c * count + k] = own_ref[k]
        rows_ref[(1 - c) * count + k] = other_ref[k]
    total = jnp.zeros((height, cols), jnp.float32)
    per_x = rows_ref.shape[0] // X
    half = per_x // 2
    for piece, weight_ref in enumerate(weight_refs):
        offset = (0, X - 1, 1, 2)[piece // 2]
        first = lax.rem(x + offset, X) * per_x + piece % 2 * half
        wide = jnp.concatenate(
            [rows_ref[first + k] for k in range(weight_ref.shape[0] // cols)], axis=1
        )
        total += jnp.dot(wide, weight_ref[...], preferred_element_type=jnp.float32)
    drafted = jnp.tanh(2.0 * total).astype(own_ref.dtype)
    if last:
        for k, earlier_ref in enumerate(earlier_refs):
            stack_ref[k] = earlier_ref[...]
        stack_ref[len(earlier_refs)] = drafted
        return
    drafted_ref[...] = drafted
    for copy in range(count):
        copies_ref[copy] = drafted
    for kept_ref, weight_ref in zip(kept_refs, weight_refs[X:]):
        kept_ref[...] = weight_ref[...]


def draft_step(own, other, weights, earlier, last, keep):
    count, height, cols = own.shape
    vmem = pl.BlockSpec(memory_space=pltpu.VMEM)
    rows = pltpu.VMEM((2 * count, height, cols), own.dtype)
    block = jax.ShapeDtypeStruct((height, cols), own.dtype)
    copies = jax.ShapeDtypeStruct(own.shape, own.dtype)
    if last:
        operands = (own, other, *weights, *earlier)
        out_shape = jax.ShapeDtypeStruct((len(earlier) + 1, height, cols), own.dtype)
        out_specs, scratch = vmem, [rows]
    else:
        operands = (own, other, *weights)
        kept = [jax.ShapeDtypeStruct(piece.shape, piece.dtype) for piece in weights[X:]]
        out_shape, scratch = [block, copies] + (kept if keep else []), [rows]
        out_specs = [vmem] * len(out_shape)
    return pl.pallas_call(
        functools.partial(draft_kernel, last=last),
        out_shape=out_shape,
        in_specs=[vmem] * len(operands),
        out_specs=out_specs,
        scratch_shapes=scratch,
        compiler_params=pltpu.CompilerParams(vmem_limit_bytes=8 << 20),
        cost_estimate=pl.CostEstimate(
            flops=4 * count * height * cols * cols,
            bytes_accessed=4 * count * cols * cols + 6 * count * height * cols,
            transcendentals=height * cols,
        ),
        name="draft_step",
    )(*operands)


def near_holders():
    pairs = []
    for yh in range(YH):
        for yl in range(YL):
            for z in range(Z):
                for x in range(X):
                    for c in range(C):
                        y = yh * YL + yl
                        near = (z // X * X + 2 * (z % X) - 2 + c) % Z
                        source = ((x * Z + near) * X + y) * C + z // X
                        pairs.append((source, ((y * Z + z) * X + x) * C + c))
    return pairs


NEAR_HOLDER = near_holders()


def accepted_of_my_windows(block, rows):
    start = lax.axis_index("dp") * rows % block.shape[0]
    return lax.dynamic_slice_in_dim(block, start, rows, 0)


def pick(rows, accepted):
    chosen = jnp.arange(rows.shape[1])[None, :] == (accepted - 1)[:, None]
    return jnp.sum(
        jnp.where(chosen[:, :, None], rows, jnp.zeros((), rows.dtype)), axis=1, dtype=rows.dtype
    )


def per_device(
    queries,
    new_keys,
    new_values,
    key_cache,
    value_cache,
    cache_lengths,
    accepted,
    residual,
    out_weight,
    draft_weight,
):
    windows_here, tokens_here, query_width = queries.shape
    cache_size = key_cache.shape[1]
    kv_here = new_keys.shape[2] // HD
    group_size = query_width // HD // kv_here
    tensor_size = lax.axis_size("tensor")
    holder_block, swapped, swapped_other = lax.optimization_barrier(
        (
            move(accepted, NEAR_HOLDER),
            move(draft_weight, SWAPPED),
            move(draft_weight, SWAPPED_OTHER),
        )
    )
    own_accepted = accepted_of_my_windows(holder_block, windows_here)

    query_split = queries.reshape(windows_here, tokens_here, kv_here, group_size, HD)
    keys_cached = key_cache.reshape(windows_here, cache_size, kv_here, HD)
    keys_fresh = new_keys.reshape(windows_here, tokens_here, kv_here, HD)
    score_cache = jnp.einsum(
        "wtkgd,wpkd->wkgtp", query_split, keys_cached, preferred_element_type=jnp.float32
    ) * HD ** (-0.5)
    score_fresh = jnp.einsum(
        "wtkgd,wpkd->wkgtp", query_split, keys_fresh, preferred_element_type=jnp.float32
    ) * HD ** (-0.5)
    live_cache = (jnp.arange(cache_size)[None, :] < cache_lengths[:, None])[:, None, None, None, :]
    live_fresh = jnp.arange(tokens_here)[None, :] <= jnp.arange(tokens_here)[:, None]
    scores = jnp.concatenate(
        [
            jnp.where(live_cache, score_cache, -jnp.inf),
            jnp.where(live_fresh, score_fresh, -jnp.inf),
        ],
        axis=-1,
    )
    largest = jnp.max(scores, axis=-1, keepdims=True)
    powered = jnp.exp(scores - largest)
    weights = (powered / jnp.sum(powered, axis=-1, keepdims=True)).astype(jnp.bfloat16)
    values_cached = value_cache.reshape(windows_here, cache_size, kv_here, HD)
    values_fresh = new_values.reshape(windows_here, tokens_here, kv_here, HD)
    mixed_rows = jnp.einsum(
        "wkgtp,wpkd->wtkgd",
        weights[..., :cache_size],
        values_cached,
        preferred_element_type=jnp.float32,
    )
    mixed_rows = mixed_rows + jnp.einsum(
        "wkgtp,wpkd->wtkgd",
        weights[..., cache_size:],
        values_fresh,
        preferred_element_type=jnp.float32,
    )
    attended = mixed_rows.astype(jnp.bfloat16).reshape(windows_here, tokens_here, query_width)

    picked = pick(attended, own_accepted)
    low_half = lax.axis_index("dp") < YL * Z
    top = jnp.where(low_half, swapped, swapped_other)
    bottom = jnp.where(low_half, swapped_other, swapped)
    top_left, bottom_right = move(top, FROM_LEFT), move(bottom, FROM_RIGHT)
    picked_rows = spread(picked, "dp").reshape(-1, query_width)
    bottom_left, top_right = move(bottom, FROM_LEFT), move(top, FROM_RIGHT)
    picked_part = jnp.dot(picked_rows, out_weight, preferred_element_type=jnp.float32)
    block_windows, block_tokens, block_cols = residual.shape
    shares = lax.all_to_all(
        picked_part.astype(jnp.bfloat16).reshape(tensor_size, block_windows, block_cols),
        "tensor",
        split_axis=0,
        concat_axis=0,
        tiled=True,
    )
    shares, top_left, bottom_left, top_right, bottom_right = lax.optimization_barrier(
        (shares, top_left, bottom_left, top_right, bottom_right)
    )
    top_across, bottom_across = move(top_left, FROM_LEFT), move(bottom_right, FROM_RIGHT)
    weights = (
        top, bottom, top_left, bottom_left, top_right, bottom_right, top_across, bottom_across
    )
    current = (
        pick(residual, accepted).astype(jnp.float32) + jnp.sum(shares.astype(jnp.float32), axis=0)
    ).astype(jnp.bfloat16)

    gathered = lax.all_gather(
        attended.reshape(windows_here * tokens_here, query_width), "dp", axis=0, tiled=True
    )

    current = move(current, SWAPPED)
    copies = jnp.broadcast_to(current[None], (len(BLOCKS[0]),) + current.shape)
    results = []
    for step in range(STEPS):
        own = exchange_copies(copies)
        if step == HOLD:
            gathered, own = lax.optimization_barrier((gathered, own))
        other = move(own, OTHER_CORE)
        last = step + 1 == STEPS
        drafted = draft_step(own, other, weights, results, last, step == HOLD)
        if last:
            break
        drafted, copies, *kept = drafted
        if kept:
            weights = (*weights[:X], *kept)
        results.append(drafted)
    partial_out = jnp.dot(gathered, out_weight, preferred_element_type=jnp.float32)
    summed = lax.psum_scatter(partial_out, "tensor", scatter_dimension=0, tiled=True)
    drafted, summed = lax.optimization_barrier((drafted, summed))
    verified = (residual.astype(jnp.float32) + summed.reshape(residual.shape)).astype(jnp.bfloat16)
    return (verified, move(drafted, SWAPPED))


def solution(mesh):
    placed = (
        P("dp", None, "tensor"),
        P("dp", None, "tensor"),
        P("dp", None, "tensor"),
        P("dp", None, "tensor"),
        P("dp", None, "tensor"),
        P("dp"),
        P("tensor"),
        P("tensor", None, "dp"),
        P("tensor", "dp"),
        P("tensor", "dp"),
    )
    return jax.shard_map(
        per_device,
        mesh=mesh,
        in_specs=placed,
        out_specs=(P("tensor", None, "dp"), P(None, "tensor", "dp")),
        check_vma=False,
    )
```

```python
import functools

import jax
import jax.numpy as jnp
from jax import lax
from jax.experimental import pallas as pl
from jax.experimental.pallas import tpu as pltpu
from jax.sharding import PartitionSpec as P

HD = 128
STEPS = 5
HOLD = 1


def spread(block, axis):
    copies = jnp.broadcast_to(block[None], (lax.axis_size(axis),) + block.shape)
    return lax.all_to_all(copies, axis, split_axis=0, concat_axis=0, tiled=True)


YH, YL, Z, X, C = 2, 2, 8, 4, 2
BLOCKS = [list(range(yh * YL * Z, (yh + 1) * YL * Z)) for yh in range(YH)]


def route(source):
    pairs = []
    for yh in range(YH):
        for yl in range(YL):
            for z in range(Z):
                for x in range(X):
                    for c in range(C):
                        ends = []
                        for syh, sx, sc in (source(yh, x, c), (yh, x, c)):
                            ends.append((((syh * YL + yl) * Z + z) * X + sx % X) * C + sc)
                        pairs.append(tuple(ends))
    return pairs


SWAPPED = route(lambda yh, x, c: (c, x, yh))
SWAPPED_OTHER = route(lambda yh, x, c: (c, x, 1 - yh))
OTHER_CORE = route(lambda yh, x, c: (yh, x, 1 - c))
FROM_LEFT = route(lambda yh, x, c: (yh, x - 1, c))
FROM_RIGHT = route(lambda yh, x, c: (yh, x + 1, c))


def move(block, pairs):
    return lax.ppermute(block, ("dp", "tensor"), pairs)


def exchange_copies(copies):
    return lax.all_to_all(
        copies, "dp", split_axis=0, concat_axis=0, tiled=True, axis_index_groups=BLOCKS
    )


def draft_kernel(own_ref, other_ref, *refs, last):
    place = lax.axis_index("tensor")
    x, c = place // C, lax.rem(place, C)
    count, height, cols = own_ref.shape
    weight_refs, refs = refs[: 2 * X], refs[2 * X :]
    if last:
        *earlier_refs, stack_ref, rows_ref = refs
    else:
        drafted_ref, copies_ref, *kept_refs, rows_ref = refs
    for k in range(count):
        rows_ref[c * count + k] = own_ref[k]
        rows_ref[(1 - c) * count + k] = other_ref[k]
    total = jnp.zeros((height, cols), jnp.float32)
    per_x = rows_ref.shape[0] // X
    half = per_x // 2
    for piece, weight_ref in enumerate(weight_refs):
        offset = (0, X - 1, 1, 2)[piece // 2]
        first = lax.rem(x + offset, X) * per_x + piece % 2 * half
        wide = jnp.concatenate(
            [rows_ref[first + k] for k in range(weight_ref.shape[0] // cols)], axis=1
        )
        total += jnp.dot(wide, weight_ref[...], preferred_element_type=jnp.float32)
    drafted = jnp.tanh(2.0 * total).astype(own_ref.dtype)
    if last:
        for k, earlier_ref in enumerate(earlier_refs):
            stack_ref[k] = earlier_ref[...]
        stack_ref[len(earlier_refs)] = drafted
        return
    drafted_ref[...] = drafted
    for copy in range(count):
        copies_ref[copy] = drafted
    for kept_ref, weight_ref in zip(kept_refs, weight_refs[X:]):
        kept_ref[...] = weight_ref[...]


def draft_step(own, other, weights, earlier, last, keep):
    count, height, cols = own.shape
    vmem = pl.BlockSpec(memory_space=pltpu.VMEM)
    rows = pltpu.VMEM((2 * count, height, cols), own.dtype)
    block = jax.ShapeDtypeStruct((height, cols), own.dtype)
    copies = jax.ShapeDtypeStruct(own.shape, own.dtype)
    if last:
        operands = (own, other, *weights, *earlier)
        out_shape = jax.ShapeDtypeStruct((len(earlier) + 1, height, cols), own.dtype)
        out_specs, scratch = vmem, [rows]
    else:
        operands = (own, other, *weights)
        kept = [jax.ShapeDtypeStruct(piece.shape, piece.dtype) for piece in weights[X:]]
        out_shape, scratch = [block, copies] + (kept if keep else []), [rows]
        out_specs = [vmem] * len(out_shape)
    return pl.pallas_call(
        functools.partial(draft_kernel, last=last),
        out_shape=out_shape,
        in_specs=[vmem] * len(operands),
        out_specs=out_specs,
        scratch_shapes=scratch,
        compiler_params=pltpu.CompilerParams(vmem_limit_bytes=8 << 20),
        cost_estimate=pl.CostEstimate(
            flops=4 * count * height * cols * cols,
            bytes_accessed=4 * count * cols * cols + 6 * count * height * cols,
            transcendentals=height * cols,
        ),
        name="draft_step",
    )(*operands)


def near_holders():
    pairs = []
    for yh in range(YH):
        for yl in range(YL):
            for z in range(Z):
                for x in range(X):
                    for c in range(C):
                        y = yh * YL + yl
                        near = (z // X * X + 2 * (z % X) - 2 + c) % Z
                        source = ((x * Z + near) * X + y) * C + z // X
                        pairs.append((source, ((y * Z + z) * X + x) * C + c))
    return pairs


NEAR_HOLDER = near_holders()


def accepted_of_my_windows(block, rows):
    start = lax.axis_index("dp") * rows % block.shape[0]
    return lax.dynamic_slice_in_dim(block, start, rows, 0)


def pick(rows, accepted):
    chosen = jnp.arange(rows.shape[1])[None, :] == (accepted - 1)[:, None]
    return jnp.sum(
        jnp.where(chosen[:, :, None], rows, jnp.zeros((), rows.dtype)), axis=1, dtype=rows.dtype
    )


def per_device(
    queries,
    new_keys,
    new_values,
    key_cache,
    value_cache,
    cache_lengths,
    accepted,
    residual,
    out_weight,
    draft_weight,
):
    windows_here, tokens_here, query_width = queries.shape
    cache_size = key_cache.shape[1]
    kv_here = new_keys.shape[2] // HD
    group_size = query_width // HD // kv_here
    tensor_size = lax.axis_size("tensor")
    holder_block, swapped, swapped_other = lax.optimization_barrier(
        (
            move(accepted, NEAR_HOLDER),
            move(draft_weight, SWAPPED),
            move(draft_weight, SWAPPED_OTHER),
        )
    )
    own_accepted = accepted_of_my_windows(holder_block, windows_here)

    query_split = queries.reshape(windows_here, tokens_here, kv_here, group_size, HD)
    keys_cached = key_cache.reshape(windows_here, cache_size, kv_here, HD)
    keys_fresh = new_keys.reshape(windows_here, tokens_here, kv_here, HD)
    score_cache = jnp.einsum(
        "wtkgd,wpkd->wkgtp", query_split, keys_cached, preferred_element_type=jnp.float32
    ) * HD ** (-0.5)
    score_fresh = jnp.einsum(
        "wtkgd,wpkd->wkgtp", query_split, keys_fresh, preferred_element_type=jnp.float32
    ) * HD ** (-0.5)
    live_cache = (jnp.arange(cache_size)[None, :] < cache_lengths[:, None])[:, None, None, None, :]
    live_fresh = jnp.arange(tokens_here)[None, :] <= jnp.arange(tokens_here)[:, None]
    scores = jnp.concatenate(
        [
            jnp.where(live_cache, score_cache, -jnp.inf),
            jnp.where(live_fresh, score_fresh, -jnp.inf),
        ],
        axis=-1,
    )
    largest = jnp.max(scores, axis=-1, keepdims=True)
    powered = jnp.exp(scores - largest)
    weights = (powered / jnp.sum(powered, axis=-1, keepdims=True)).astype(jnp.bfloat16)
    values_cached = value_cache.reshape(windows_here, cache_size, kv_here, HD)
    values_fresh = new_values.reshape(windows_here, tokens_here, kv_here, HD)
    mixed_rows = jnp.einsum(
        "wkgtp,wpkd->wtkgd",
        weights[..., :cache_size],
        values_cached,
        preferred_element_type=jnp.float32,
    )
    mixed_rows = mixed_rows + jnp.einsum(
        "wkgtp,wpkd->wtkgd",
        weights[..., cache_size:],
        values_fresh,
        preferred_element_type=jnp.float32,
    )
    attended = mixed_rows.astype(jnp.bfloat16).reshape(windows_here, tokens_here, query_width)

    picked = pick(attended, own_accepted)
    low_half = lax.axis_index("dp") < YL * Z
    top = jnp.where(low_half, swapped, swapped_other)
    bottom = jnp.where(low_half, swapped_other, swapped)
    top_left, bottom_right = move(top, FROM_LEFT), move(bottom, FROM_RIGHT)
    picked_rows = spread(picked, "dp").reshape(-1, query_width)
    bottom_left, top_right = move(bottom, FROM_LEFT), move(top, FROM_RIGHT)
    picked_part = jnp.dot(picked_rows, out_weight, preferred_element_type=jnp.float32)
    block_windows, block_tokens, block_cols = residual.shape
    shares = lax.all_to_all(
        picked_part.astype(jnp.bfloat16).reshape(tensor_size, block_windows, block_cols),
        "tensor",
        split_axis=0,
        concat_axis=0,
        tiled=True,
    )
    shares, top_left, bottom_left, top_right, bottom_right = lax.optimization_barrier(
        (shares, top_left, bottom_left, top_right, bottom_right)
    )
    top_across, bottom_across = move(top_left, FROM_LEFT), move(bottom_right, FROM_RIGHT)
    weights = (
        top, bottom, top_left, bottom_left, top_right, bottom_right, top_across, bottom_across
    )
    current = (
        pick(residual, accepted).astype(jnp.float32) + jnp.sum(shares.astype(jnp.float32), axis=0)
    ).astype(jnp.bfloat16)

    gathered = lax.all_gather(
        attended.reshape(windows_here * tokens_here, query_width), "dp", axis=0, tiled=True
    )

    current = move(current, SWAPPED)
    copies = jnp.broadcast_to(current[None], (len(BLOCKS[0]),) + current.shape)
    results = []
    for step in range(STEPS):
        own = exchange_copies(copies)
        if step == HOLD:
            gathered, own = lax.optimization_barrier((gathered, own))
        other = move(own, OTHER_CORE)
        last = step + 1 == STEPS
        drafted = draft_step(own, other, weights, results, last, step == HOLD)
        if last:
            break
        drafted, copies, *kept = drafted
        if kept:
            weights = (*weights[:X], *kept)
        results.append(drafted)
    partial_out = jnp.dot(gathered, out_weight, preferred_element_type=jnp.float32)
    summed = lax.psum_scatter(partial_out, "tensor", scatter_dimension=0, tiled=True)
    verified = (residual.astype(jnp.float32) + summed.reshape(residual.shape)).astype(jnp.bfloat16)
    return (verified, move(drafted, SWAPPED))


def solution(mesh):
    placed = (
        P("dp", None, "tensor"),
        P("dp", None, "tensor"),
        P("dp", None, "tensor"),
        P("dp", None, "tensor"),
        P("dp", None, "tensor"),
        P("dp"),
        P("tensor"),
        P("tensor", None, "dp"),
        P("tensor", "dp"),
        P("tensor", "dp"),
    )
    return jax.shard_map(
        per_device,
        mesh=mesh,
        in_specs=placed,
        out_specs=(P("tensor", None, "dp"), P(None, "tensor", "dp")),
        check_vma=False,
    )
```
